128 devices in a mesh: shot: 32 (over y, x_lo, z), slab: 4 (over x_hi, core).
Axes of the slice: x: 4 (x_hi: 2, x_lo: 2; x = x_hi * 2 + x_lo), y: 4, z: 4, core: 2. Of those that a mesh axis runs over, the one named last changes fastest.
Arguments:
- forward_state: float32 [32, 9, 32, 32, 128], P('shot', None, 'slab'), may hold values from -6 to 6
- adjoint_state: float32 [32, 9, 32, 32, 128], P('shot', None, 'slab'), may hold values from -6 to 6
- materials: float32 [10, 32, 32, 128], P(None, 'slab', 'shot'), may hold values from 0.1 to 2, as said below
- wavelet: float32 [4], replicated, may hold values from -4 to 4
- encoding: int32 [32, 16], P('shot'), may hold values from 0 to 1
- source_cells: int32 [32, 16], P('shot'), may hold values from 0 to 131071
- receiver_depth: int32 [32, 32], P('slab'), may hold values from 0 to 3
- receiver_data: float32 [32, 4, 32, 32], P('shot', None, 'slab'), may hold values from -6 to 6
Outputs:
- forward_out: float32 [32, 9, 32, 32, 128], P('shot', None, 'slab')
- adjoint_out: float32 [32, 9, 32, 32, 128], P('shot', None, 'slab')
- gradient: float32 [10, 32, 32, 128], P(None, 'slab', 'shot')
The draws below stay inside these ranges and needn't reach their ends.
Inputs may be any that keep to these rules, and one draw needn't show every extreme that they name: `materials`: row 0 lies in 0.5 to 1; rows 1, 4, 6 in 1 to 2; rows 2, 3, 5 in 0.1 to 0.4; rows 7, 8, 9 in 0.3 to 1.
All inputs are finite; a program needn't handle non-finite values.
Results may differ from the reference program's by a relative error of at most 0.0001.
Values sent between devices are 32-bit elements; how exact they have to be, the bound alone decides.
No kernel may reach another device: no remote copies, remote signals or barrier semaphores. Data moves between devices by JAX's collectives and lax.ppermute only.
A program may use at most 64 MiB of HBM per device.

```python
import jax
import jax.numpy as jnp
from jax import lax

NY = 32
NZ = 128
NSRC = 16
STEPS = 4
SHOTS = 32
NX = 32


def draw_materials(key, part):
    lower_ends = jnp.array([0.5, 1.0, 0.1, 0.1, 1.0, 0.1, 1.0, 0.3, 0.3, 0.3], jnp.float32)[:, None, None, None]
    upper_ends = jnp.array([1.0, 2.0, 0.4, 0.4, 2.0, 0.4, 2.0, 1.0, 1.0, 1.0], jnp.float32)[:, None, None, None]
    uniform_draw = jax.random.uniform(key, (10, NX, NY, NZ), jnp.float32)
    return lower_ends * (upper_ends / lower_ends) ** uniform_draw


def touch_ends(result, key, low, high):
    index_at = [jax.random.randint(jax.random.fold_in(key, axis), (), 0, length) for axis, length in enumerate(result.shape)]
    widest = result.shape.index(max(result.shape))
    neighbour = index_at[:widest] + [(index_at[widest] + 1) % result.shape[widest]] + index_at[widest + 1:]
    return result.at[tuple(index_at)].set(low).at[tuple(neighbour)].set(high)


def level_of(key, shape, pieces, least, top_value):
    level, own = 1.0, jax.random.fold_in(key, 6)
    for axis_at, parts in pieces:
        draws = jnp.exp(jax.random.uniform(jax.random.fold_in(own, axis_at), (parts,), jnp.float32, least / len(pieces), top_value / len(pieces)))
        level = level * jnp.repeat(draws, shape[axis_at] // parts).reshape([-1 if axis == axis_at else 1 for axis in range(len(shape))])
    return level


def centred(own_key, shape, deviation, reach, pieces=(), held_as=jnp.bfloat16):
    result = jax.random.normal(own_key, shape, jnp.float32) * deviation
    if len(pieces) > 0:
        result = level_of(own_key, shape, pieces, -0.22, 0.18) * result
    return jnp.clip(result, min=-reach, max=reach).astype(held_as)


def setup_inputs(seed: int = 0) -> dict:
    splits = jax.random.split(jax.random.key(seed), 9)
    return {
        "forward_state": centred(splits[0], (SHOTS, 9, NX, NY, NZ), 1.0, 6.0, ((0, 32), (2, 4)), jnp.float32),
        "adjoint_state": centred(splits[1], (SHOTS, 9, NX, NY, NZ), 1.0, 6.0, ((0, 32), (2, 4)), jnp.float32),
        "materials": draw_materials(jax.random.fold_in(splits[8], 71), 0),
        "wavelet": centred(splits[3], (STEPS,), 1.0, 4.0, (), jnp.float32),
        "encoding": touch_ends(jax.random.randint(splits[4], (SHOTS, NSRC), 0, 2), jax.random.fold_in(splits[4], 1), 0, 1).astype(jnp.int32),
        "source_cells": touch_ends(jax.random.randint(splits[5], (SHOTS, NSRC), 0, NX * NY * NZ), jax.random.fold_in(splits[5], 1), 0, (NX * NY * NZ) - 1).astype(jnp.int32),
        "receiver_depth": touch_ends(jax.random.randint(splits[6], (NX, NY), 0, 4), jax.random.fold_in(splits[6], 1), 0, 3).astype(jnp.int32),
        "receiver_data": centred(splits[7], (SHOTS, STEPS, NX, NY), 1.0, 6.0, ((0, 32), (2, 4)), jnp.float32),
    }


step_size = 0.25


def diff_up(values, direction):
    length = values.shape[direction]
    ahead = lax.slice_in_dim(values, 1, length, axis=direction)
    zero_layer = jnp.zeros_like(lax.slice_in_dim(values, 0, 1, axis=direction))
    return jnp.concatenate([ahead, zero_layer], axis=direction) - values


def diff_down(values, direction):
    length = values.shape[direction]
    behind = lax.slice_in_dim(values, 0, length - 1, axis=direction)
    zero_layer = jnp.zeros_like(lax.slice_in_dim(values, 0, 1, axis=direction))
    return values - jnp.concatenate([zero_layer, behind], axis=direction)


def velocity_forces(stress, dx_sxx, dx_sxy, dx_sxz):
    force_x = dx_sxx + diff_down(stress[:, 5], 2) + diff_down(stress[:, 4], 3)
    force_y = dx_sxy + diff_up(stress[:, 1], 2) + diff_down(stress[:, 3], 3)
    force_z = dx_sxz + diff_down(stress[:, 3], 2) + diff_up(stress[:, 2], 3)
    return jnp.stack([force_x, force_y, force_z], axis=1)


def strains(velocity, dx_vx, dx_vy, dx_vz):
    strain_xx = dx_vx
    strain_yy = diff_down(velocity[:, 1], 2)
    strain_zz = diff_down(velocity[:, 2], 3)
    strain_yz = diff_up(velocity[:, 1], 3) + diff_up(velocity[:, 2], 2)
    strain_xz = diff_up(velocity[:, 0], 3) + dx_vz
    strain_xy = diff_up(velocity[:, 0], 2) + dx_vy
    return [strain_xx, strain_yy, strain_zz, strain_yz, strain_xz, strain_xy]


def stress_rates(strain, stiffness):
    strain_xx, strain_yy, strain_zz, strain_yz, strain_xz, strain_xy = strain
    return jnp.stack([
        stiffness[0] * strain_xx + stiffness[1] * strain_yy + stiffness[2] * strain_zz,
        stiffness[1] * strain_xx + stiffness[3] * strain_yy + stiffness[4] * strain_zz,
        stiffness[2] * strain_xx + stiffness[4] * strain_yy + stiffness[5] * strain_zz,
        stiffness[6] * strain_yz,
        stiffness[7] * strain_xz,
        stiffness[8] * strain_xy], axis=1)


def correlate(buoy_grad, strain, halfway):
    forward = [part[:halfway] for part in strain]
    adjoint = [part[halfway:] for part in strain]
    pairs = [(0, 0), (0, 1), (0, 2), (1, 1), (1, 2), (2, 2), (3, 3), (4, 4), (5, 5)]
    terms = [buoy_grad]
    for first, second in pairs:
        product = forward[first] * adjoint[second]
        if first != second:
            product = product + forward[second] * adjoint[first]
        terms.append(jnp.sum(product, axis=0))
    return jnp.stack(terms)


def reference(forward_state, adjoint_state, materials, wavelet, encoding, source_cells, receiver_depth, receiver_data):
    cell_count = NX * NY * NZ
    probe = (lax.broadcasted_iota(jnp.int32, (NX, NY, NZ), 2) == receiver_depth[:, :, None]).astype(jnp.float32)
    buoyancy = materials[0]
    stiffness = materials[1:]

    def one_shot(grad_total, inputs):
        forward, adjoint, shot_code, shot_cells, shot_data = inputs
        sign_values = (2 * shot_code - 1).astype(jnp.float32)
        source_image = jnp.zeros((cell_count,), jnp.float32).at[shot_cells].add(sign_values).reshape(NX, NY, NZ)
        state = jnp.stack([forward, adjoint])
        velocity = state[:, 0:3]
        stress = state[:, 3:9]
        for step_index in range(STEPS):
            force = velocity_forces(stress, diff_up(stress[:, 0], 1), diff_down(stress[:, 5], 1), diff_down(stress[:, 4], 1))
            buoy_grad = jnp.sum(force[0:1] * velocity[1:2], axis=(0, 1))
            velocity = velocity + step_size * buoyancy * force
            strain = strains(velocity, diff_down(velocity[:, 0], 1), diff_up(velocity[:, 1], 1), diff_up(velocity[:, 2], 1))
            stress = stress + step_size * stress_rates(strain, stiffness)
            inject = jnp.stack([wavelet[step_index] * source_image, shot_data[step_index][:, :, None] * probe])
            stress = stress.at[:, 2].add(inject)
            grad_total = grad_total + correlate(buoy_grad, strain, 1)
        state = jnp.concatenate([velocity, stress], axis=1)
        return grad_total, (state[0], state[1])

    start = jnp.zeros((10, NX, NY, NZ), jnp.float32)
    grad_total, outputs = lax.scan(one_shot, start, (forward_state, adjoint_state, encoding, source_cells, receiver_data))
    gradient = grad_total * (float(SHOTS * STEPS) ** -0.5)
    return outputs[0], outputs[1], gradient
```

```python
import functools

import jax
import jax.numpy as jnp
from jax import lax
from jax.experimental import pallas as pl
from jax.experimental.pallas import tpu as pltpu
from jax.sharding import PartitionSpec as P

STEPS = 4
DEPTH = 2
OWN = 8
VX, VY, VZ, SXX, SYY, SZZ, SYZ, SXZ, SXY = range(9)
step_size = 0.25
VMEM = pltpu.VMEM
SMEM = pltpu.SMEM


def phase_kernel(depth, y_rows, z_rows, steps, first, last, *refs):
    refs = list(refs)
    wavelet, state_in = refs.pop(0), refs.pop(0)
    if first:
        own_rows, rim_rows = refs.pop(0), refs.pop(0)
    else:
        halo_lo, halo_hi, mats, acc_in = (refs.pop(0) for slot in range(4))
    image, data = refs.pop(0), refs.pop(0)
    state, acc = refs.pop(0), refs.pop(0)
    if first:
        mats = refs.pop(0)
    if last:
        packed = refs.pop(0)
    else:
        send_dn, send_up = refs.pop(0), refs.pop(0)

    length = OWN + 2 * depth
    chunks = y_rows // 8
    row = lax.broadcasted_iota(jnp.int32, (8, z_rows), 0)
    lane = lax.broadcasted_iota(jnp.int32, (8, z_rows), 1)
    row_first, row_last = row == 0, row == 7
    lane_first, lane_last = lane == 0, lane == z_rows - 1
    nought = jnp.zeros((8, z_rows), jnp.float32)

    def rows_of(c):
        return pl.ds(8 * c, 8)

    if first:
        own_count, rim_count = 10 * OWN, rim_rows.shape[0] // y_rows
        side = depth + 9 * (depth - 1)

        def take(source, count, r, c):
            return step_size * source[pl.ds(r + 8 * c * count, 8, stride=count), :]

        for c in range(chunks):
            for r in range(own_count):
                mats[r // OWN, depth + r % OWN, rows_of(c), :] = take(own_rows, own_count, r, c)
            for base, buoy_at, stiff_at in ((0, 0, 1), (side, depth + OWN, depth + OWN)):
                for j in range(depth):
                    mats[0, buoy_at + j, rows_of(c), :] = take(rim_rows, rim_count, base + j, c)
                for m in range(9):
                    for j in range(depth - 1):
                        r = base + depth + m * (depth - 1) + j
                        mats[1 + m, stiff_at + j, rows_of(c), :] = take(rim_rows, rim_count, r, c)
    else:
        for f in range(18):
            for j in range(depth):
                state[f, j] = halo_lo[f, j]
                state[f, depth + OWN + j] = halo_hi[f, j]

    def at(f, i, c):
        return state[f, i, rows_of(c), :]

    def up_y(f, i, c, a):
        b = at(f, i, c + 1) if c + 1 < chunks else nought
        return pltpu.roll(jnp.where(row_first, b, a), 7, 0) - a

    def down_y(f, i, c, a):
        b = at(f, i, c - 1) if c > 0 else nought
        return a - pltpu.roll(jnp.where(row_last, b, a), 1, 0)

    def up_z(a):
        return pltpu.roll(jnp.where(lane_first, 0.0, a), z_rows - 1, 1) - a

    def down_z(a):
        return a - pltpu.roll(jnp.where(lane_last, 0.0, a), 1, 1)

    def force(s, i, c, which):
        sxy, sxz = at(s + SXY, i, c), at(s + SXZ, i, c)
        out = [None] * 3
        if 0 in which:
            up_x = at(s + SXX, i + 1, c) - at(s + SXX, i, c)
            out[0] = up_x + down_y(s + SXY, i, c, sxy) + down_z(sxz)
        if 1 in which:
            syz = at(s + SYZ, i, c)
            syy, szz = at(s + SYY, i, c), at(s + SZZ, i, c)
            down_sxy = sxy - at(s + SXY, i - 1, c)
            down_sxz = sxz - at(s + SXZ, i - 1, c)
            out[1] = down_sxy + up_y(s + SYY, i, c, syy) + down_z(syz)
            out[2] = down_sxz + down_y(s + SYZ, i, c, syz) + up_z(szz)
        return out

    def velocity_plane(i, which, slot=None, fresh=False):
        for c in range(chunks):
            buoyancy = mats[0, i, rows_of(c), :]
            term = None
            both = [force(s, i, c, which) for s in (0, 9)]
            old = [[at(s + d, i, c) for d in range(3)] for s in (0, 9)]
            for d in which:
                for side_at, s in enumerate((0, 9)):
                    state[s + d, i, rows_of(c), :] = old[side_at][d] + buoyancy * both[side_at][d]
            if slot is not None:
                term = both[0][0] * old[1][0] + both[0][1] * old[1][1] + both[0][2] * old[1][2]
                if not fresh:
                    term = acc[0, slot, rows_of(c), :] + term
                acc[0, slot, rows_of(c), :] = term

    def strain(s, i, c):
        vx, vy, vz = at(s + VX, i, c), at(s + VY, i, c), at(s + VZ, i, c)
        return [
            vx - at(s + VX, i - 1, c),
            down_y(s + VY, i, c, vy),
            down_z(vz),
            up_z(vy) + up_y(s + VZ, i, c, vz),
            up_z(vx) + (at(s + VZ, i + 1, c) - vz),
            up_y(s + VX, i, c, vx) + (at(s + VY, i + 1, c) - vy),
        ]

    def stress_plane(i, step, slot=None, fresh=False, final=False):
        for c in range(chunks):
            m = [None] + [mats[k, i, rows_of(c), :] for k in range(1, 10)]
            both = []
            for s in (0, 9):
                e = strain(s, i, c)
                both.append(e)
                if s == 0:
                    inject = wavelet[step] * image[i, rows_of(c), :]
                else:
                    inject = data[step, i, rows_of(c), :]
                rates = [
                    m[1] * e[0] + m[2] * e[1] + m[3] * e[2],
                    m[2] * e[0] + m[4] * e[1] + m[5] * e[2],
                    m[3] * e[0] + m[5] * e[1] + m[6] * e[2] + inject,
                    m[7] * e[3],
                    m[8] * e[4],
                    m[9] * e[5],
                ]
                for f, rate in enumerate(rates):
                    state[s + SXX + f, i, rows_of(c), :] = at(s + SXX + f, i, c) + rate
            if slot is None:
                continue
            f, a = both
            terms = [
                f[0] * a[0],
                f[0] * a[1] + f[1] * a[0],
                f[0] * a[2] + f[2] * a[0],
                f[1] * a[1],
                f[1] * a[2] + f[2] * a[1],
                f[2] * a[2],
                f[3] * a[3],
                f[4] * a[4],
                f[5] * a[5],
            ]
            for n, term in enumerate(terms):
                if not fresh:
                    term = acc[1 + n, slot, rows_of(c), :] + term
                if final:
                    packed[pl.ds((1 + n) * OWN + slot + 8 * c * 10 * OWN, 8, stride=10 * OWN), :] = term
                else:
                    acc[1 + n, slot, rows_of(c), :] = term
            if final:
                packed[pl.ds(slot + 8 * c * 10 * OWN, 8, stride=10 * OWN), :] = acc[0, slot, rows_of(c), :]

    for at_step, step in enumerate(steps):
        shrink = at_step + 1
        fresh = first and at_step == 0
        final = last and shrink == depth
        velocity_plane(shrink - 1, (0,))
        for i in range(shrink, depth):
            velocity_plane(i, (0, 1, 2))

        def velocity_own(x, carry):
            velocity_plane(depth + x, (0, 1, 2), x, fresh)
            return carry

        lax.fori_loop(0, OWN, velocity_own, 0)
        for i in range(depth + OWN, length - shrink):
            velocity_plane(i, (0, 1, 2))
        velocity_plane(length - shrink, (1, 2))
        for i in range(shrink, depth):
            stress_plane(i, step)

        def stress_own(x, carry):
            stress_plane(depth + x, step, x, fresh, final)
            return carry

        lax.fori_loop(0, OWN, stress_own, 0)
        for i in range(depth + OWN, length - shrink):
            stress_plane(i, step)

    if not last:
        for f in range(18):
            for j in range(depth):
                send_dn[f, j] = state[f, depth + j]
                send_up[f, j] = state[f, OWN + j]


def run_phase(steps, first, last, wavelet, state, extra, image, data):
    fields, length, y_rows, z_rows = state.shape
    depth = (length - OWN) // 2
    whole = pl.BlockSpec(memory_space=VMEM)
    outs = [
        VMEM(state.shape, jnp.float32),
        VMEM((10, OWN, y_rows, z_rows), jnp.float32),
    ]
    aliases = {1: 0}
    if first:
        outs.append(VMEM((10, length, y_rows, z_rows), jnp.float32))
    else:
        aliases[5] = 1
    if last:
        outs.append(VMEM((y_rows * 10 * OWN, z_rows), jnp.float32))
    else:
        outs += [VMEM((fields, depth, y_rows, z_rows), jnp.float32)] * 2
    cells = (OWN + depth) * y_rows * z_rows * len(steps)
    return pl.pallas_call(
        functools.partial(phase_kernel, depth, y_rows, z_rows, steps, first, last),
        out_shape=tuple(outs),
        in_specs=[pl.BlockSpec(memory_space=SMEM)] + [whole] * (3 + len(extra)),
        out_specs=tuple([whole] * len(outs)),
        input_output_aliases=aliases,
        cost_estimate=pl.CostEstimate(flops=160 * cells, bytes_accessed=8 * cells, transcendentals=0),
        compiler_params=pltpu.CompilerParams(vmem_limit_bytes=4 << 20),
        name="phase",
    )(wavelet, *[pltpu.with_memory_space_constraint(x, VMEM) for x in (state, *extra, image, data)])


def to_next(value):
    peers = lax.axis_size("slab")
    return lax.ppermute(value, "slab", [(i, i + 1) for i in range(peers - 1)])


def to_previous(value):
    peers = lax.axis_size("slab")
    return lax.ppermute(value, "slab", [(i + 1, i) for i in range(peers - 1)])


def gather_rows(rows):
    copies = jnp.broadcast_to(rows, (lax.axis_size("shot"), *rows.shape))
    return lax.all_to_all(copies, "shot", split_axis=0, concat_axis=0, tiled=True)


def make_image(encoding, source_cells, start_cell, layers, y_rows, z_rows):
    span = layers * y_rows * z_rows
    local_cell = source_cells - start_cell
    inside = (local_cell >= 0) & (local_cell < span)
    target = jnp.where(inside, local_cell, span)
    signs = (2 * encoding - 1).astype(jnp.float32)
    image = jnp.zeros((span,), jnp.float32).at[target].add(signs, mode="drop")
    return image.reshape(layers, y_rows, z_rows)


def body(
    forward_state,
    adjoint_state,
    materials,
    wavelet,
    encoding,
    source_cells,
    receiver_depth,
    receiver_data,
):
    _, comps, own, y_rows, z_rows = forward_state.shape
    k = DEPTH
    length = own + 2 * k
    mats = materials.reshape(10, own, z_rows)
    own_rows = gather_rows(mats.reshape(10 * own, z_rows))

    recv = jnp.concatenate([receiver_data[0], receiver_depth.astype(jnp.float32)[None]], axis=0)
    tail = -(-5 * k * y_rows // z_rows)

    def rim_of(buoy_from, stiff_from):
        buoy = mats[0, buoy_from : buoy_from + k]
        stiff = mats[1:, stiff_from : stiff_from + k - 1].reshape(9 * (k - 1), z_rows)
        line = recv[:, buoy_from : buoy_from + k].reshape(-1)
        line = jnp.pad(line, (0, tail * z_rows - line.shape[0])).reshape(tail, z_rows)
        return jnp.concatenate([buoy, stiff, line], axis=0)

    side = k + 9 * (k - 1)
    rim_lo = to_next(rim_of(own - k, own - k + 1))
    rim_hi = to_previous(rim_of(0, 0))
    rim_rows = jnp.concatenate([rim_lo[:side], rim_hi[:side]], axis=0)
    rim_rows = jnp.pad(rim_rows, ((0, -2 * side % 8), (0, 0)))
    rim_rows = gather_rows(rim_rows)

    def recv_of(rim):
        return rim[side:].reshape(-1)[: 5 * k * y_rows].reshape(5, k, y_rows)

    recv = jnp.concatenate([recv_of(rim_lo), recv, recv_of(rim_hi)], axis=1)
    z_at = lax.broadcasted_iota(jnp.int32, (1, length, y_rows, z_rows), 3).astype(jnp.float32)
    data = jnp.where(z_at == recv[4:5, :, :, None], recv[:4, :, :, None], 0.0)
    start_cell = (lax.axis_index("slab") * own - k) * (y_rows * z_rows)
    image = make_image(encoding[0], source_cells[0], start_cell, length, y_rows, z_rows)

    both = [forward_state[0], adjoint_state[0]]
    halo_lo = to_next(jnp.concatenate([part[:, own - k :] for part in both], axis=0))
    halo_hi = to_previous(jnp.concatenate([part[:, :k] for part in both], axis=0))
    state = jnp.concatenate([halo_lo, jnp.concatenate(both, axis=0), halo_hi], axis=1)

    def flat(rows):
        return rows.reshape(-1, z_rows)

    phases = STEPS // k
    extra = (flat(own_rows), flat(rim_rows))
    for p in range(phases):
        first, last = p == 0, p == phases - 1
        steps = tuple(range(p * k, p * k + k))
        outs = list(run_phase(steps, first, last, wavelet, state, extra, image, data))
        state, acc = outs.pop(0), outs.pop(0)
        if first:
            stored = outs.pop(0)
        if last:
            packed = outs.pop(0)
        else:
            extra = (to_next(outs.pop(1)), to_previous(outs.pop(0)), stored, acc)

    packed = packed.reshape(y_rows, 10 * own, z_rows)
    tiles = lax.all_to_all(packed, "shot", 0, 0, tiled=True)
    shots = lax.axis_size("shot")
    gradient = jnp.sum(tiles, axis=0) * float(shots * STEPS) ** (-0.5)
    gradient = gradient.reshape(10, own, 1, z_rows)
    forward_out = state[None, :comps, k : k + own]
    adjoint_out = state[None, comps:, k : k + own]
    return forward_out, adjoint_out, gradient


def solution(mesh):
    state_spec = P("shot", None, "slab", None, None)
    return jax.shard_map(
        body,
        mesh=mesh,
        in_specs=(
            state_spec,
            state_spec,
            P(None, "slab", "shot", None),
            P(),
            P("shot", None),
            P("shot", None),
            P("slab", None),
            P("shot", None, "slab", None),
        ),
        out_specs=(state_spec, state_spec, P(None, "slab", "shot", None)),
        check_vma=False,
    )
```

```python
import functools

import jax
import jax.numpy as jnp
from jax import lax
from jax.experimental import pallas as pl
from jax.experimental.pallas import tpu as pltpu
from jax.sharding import PartitionSpec as P

STEPS = 4
DEPTH = 2
OWN = 8
LENGTH = OWN + 2 * DEPTH
VX, VY, VZ, SXX, SYY, SZZ, SYZ, SXZ, SXY = range(9)
step_size = 0.25
VMEM = pltpu.VMEM
ROWS = 104

BOTH = (SXX, SXY, SXZ)
UP = [(VX, OWN - 2), (VY, OWN - 1), (VZ, OWN - 1)]
UP += [(f, OWN - 2) for f in BOTH] + [(f, OWN - 1) for f in range(SXX, SXY + 1)]
DOWN = [(VX, 0), (VY, 1), (VZ, 1)] + [(f, j) for f in range(SXX, SXY + 1) for j in (0, 1)]
UP_FIRST = UP + [(VX, OWN - 1)]
DOWN_FIRST = DOWN + [(VY, 0), (VZ, 0)]


def sizes(first):
    up, down = (UP_FIRST, DOWN_FIRST) if first else (UP, DOWN)
    return up, down, 2 * max(len(up), len(down))


def is_odd():
    return lax.rem(lax.axis_index("slab"), 2) == 1


def fill_payloads(first, state, cross, chip, data=None):
    up, down, base = sizes(first)

    def fill(target, planes, layer):
        for s in range(2):
            for n, (f, j) in enumerate(planes):
                target[s * len(planes) + n] = state[9 * s + f, DEPTH + j]
        if data is not None:
            for n in range(STEPS // DEPTH):
                target[base + n] = data[n * DEPTH, layer]

    @pl.when(is_odd())
    def _():
        fill(cross, up, OWN - 1)
        fill(chip, down, 0)

    @pl.when(jnp.logical_not(is_odd()))
    def _():
        fill(cross, down, 0)
        fill(chip, up, OWN - 1)


RIM = (((VY, 0), (VZ, 0)), ((VX, LENGTH - 1), (9 + VX, LENGTH - 1)))


def drain_payloads(first, state, cross, chip):
    up, down, base = sizes(first)

    def drain(source, planes, shift, at):
        for s in range(2):
            for n, (f, j) in enumerate(planes):
                state[9 * s + f, DEPTH + j + shift] = source[s * len(planes) + n]
        if first:
            for n, place in enumerate(RIM[at]):
                state[place] = source[base + n]

    @pl.when(is_odd())
    def _():
        drain(chip, up, -OWN, 0)
        drain(cross, down, OWN, 1)

    @pl.when(jnp.logical_not(is_odd()))
    def _():
        drain(cross, up, -OWN, 0)
        drain(chip, down, OWN, 1)


def edges_kernel(materials, own, far, near, sem):
    copy = pltpu.make_async_copy(materials, own, sem)
    copy.start()
    copy.wait()

    def take(target, layer):
        for m in range(10):
            target[pl.ds(DEPTH * m, DEPTH), :] = own[pl.ds(OWN * m + layer, DEPTH), :]

    @pl.when(is_odd())
    def _():
        take(far, OWN - DEPTH)
        take(near, 0)

    @pl.when(jnp.logical_not(is_odd()))
    def _():
        take(far, 0)
        take(near, OWN - DEPTH)


def spread_kernel(own, cross, chip, out, block, sem):
    block[pl.ds(0, 10 * OWN), :] = own[...]
    block[pl.ds(10 * OWN, ROWS - 10 * OWN), :] = jnp.zeros((ROWS - 10 * OWN, own.shape[1]), jnp.float32)
    side = DEPTH + 9

    def put(source, base, inner):
        block[pl.ds(base, DEPTH), :] = source[pl.ds(0, DEPTH), :]
        for m in range(9):
            block[pl.ds(base + DEPTH + m, 1), :] = source[pl.ds(DEPTH * (1 + m) + inner, 1), :]

    @pl.when(is_odd())
    def _():
        put(chip, 10 * OWN, DEPTH - 1)
        put(cross, 10 * OWN + side, 0)

    @pl.when(jnp.logical_not(is_odd()))
    def _():
        put(cross, 10 * OWN, DEPTH - 1)
        put(chip, 10 * OWN + side, 0)

    copies = [pltpu.make_async_copy(block, out.at[j], sem.at[j]) for j in range(out.shape[0])]
    for copy in copies:
        copy.start()
    for copy in copies:
        copy.wait()


def stage_kernel(forward, adjoint, data, state, cross, chip, sems):
    inner = pl.ds(DEPTH, OWN)
    copies = [
        pltpu.make_async_copy(part.at[f], state.at[9 * s + f, inner], sems.at[9 * s + f])
        for s, part in enumerate((forward, adjoint))
        for f in range(9)
    ]
    for copy in copies:
        copy.start()
    for copy in copies:
        copy.wait()
    fill_payloads(True, state, cross, chip, data)


def join_kernel(state_in, cross, chip, state):
    drain_payloads(True, state, cross, chip)


def draw_image(encoding, cells, image):
    layers, y_rows, z_rows = image.shape
    image[...] = jnp.zeros(image.shape, jnp.float32)
    lane = lax.broadcasted_iota(jnp.int32, (1, z_rows), 1)
    first_x = lax.axis_index("slab") * OWN - DEPTH
    for n in range(cells.shape[1]):
        cell = cells[0, n]
        x = cell // (y_rows * z_rows) - first_x
        inside = jnp.logical_and(x >= 0, x < layers)
        x = jnp.where(inside, x, 0)
        y = lax.rem(cell // z_rows, y_rows)
        sign = jnp.where(inside, 2 * encoding[0, n] - 1, 0).astype(jnp.float32)
        spot = jnp.where(lane == lax.rem(cell, z_rows), sign, 0.0)
        image[x, pl.ds(y, 1), :] = image[x, pl.ds(y, 1), :] + spot


def phase_kernel(first, y_rows, z_rows, *refs):
    refs = list(refs)
    if first:
        wavelet, encoding, cells, _, gathered, data_in, state, acc, mats, image, cross, chip, rows_ref, data, sems = refs
    else:
        wavelet, _, _, cross_in, chip_in, mats, image, data_in, state, acc, packed, rows_ref, data, sems = refs

    chunks = y_rows // 8
    scale = float(y_rows * STEPS) ** (-0.5)
    row = lax.broadcasted_iota(jnp.int32, (8, z_rows), 0)
    lane = lax.broadcasted_iota(jnp.int32, (8, z_rows), 1)
    row_first, row_last = row == 0, row == 7
    lane_first, lane_last = lane == 0, lane == z_rows - 1
    nought = jnp.zeros((8, z_rows), jnp.float32)

    def rows_of(c):
        return pl.ds(8 * c, 8)

    if first:
        copies = [
            pltpu.make_async_copy(gathered.at[c], rows_ref.at[c], sems.at[c]) for c in range(chunks)
        ]
        for copy in copies:
            copy.start()
    start = 0 if first else DEPTH
    data_copy = pltpu.make_async_copy(data_in.at[pl.ds(start, DEPTH)], data, sems.at[chunks])
    data_copy.start()
    if not first:
        drain_payloads(False, state, cross_in, chip_in)
    if first:
        draw_image(encoding, cells, image)
        side = DEPTH + 9
        for c in range(chunks):
            copies[c].wait()

            def take(r):
                return step_size * rows_ref[c, pl.ds(r, 8, stride=ROWS), :]

            for r in range(10 * OWN):
                mats[r // OWN, DEPTH + r % OWN, rows_of(c), :] = take(r)
            for base, buoy_at, stiff_at in ((80, 0, DEPTH - 1), (80 + side, DEPTH + OWN, DEPTH + OWN)):
                for j in range(DEPTH):
                    mats[0, buoy_at + j, rows_of(c), :] = take(base + j)
                for m in range(9):
                    mats[1 + m, stiff_at, rows_of(c), :] = take(base + DEPTH + m)

    def at(f, i, c):
        return state[f, i, rows_of(c), :]

    def up_y(f, i, c, a):
        b = at(f, i, c + 1) if c + 1 < chunks else nought
        return pltpu.roll(jnp.where(row_first, b, a), 7, 0) - a

    def down_y(f, i, c, a):
        b = at(f, i, c - 1) if c > 0 else nought
        return a - pltpu.roll(jnp.where(row_last, b, a), 1, 0)

    def up_z(a):
        return pltpu.roll(jnp.where(lane_first, 0.0, a), z_rows - 1, 1) - a

    def down_z(a):
        return a - pltpu.roll(jnp.where(lane_last, 0.0, a), 1, 1)

    def force(s, i, c, which):
        sxy, sxz = at(s + SXY, i, c), at(s + SXZ, i, c)
        out = [None] * 3
        if 0 in which:
            up_x = at(s + SXX, i + 1, c) - at(s + SXX, i, c)
            out[0] = up_x + down_y(s + SXY, i, c, sxy) + down_z(sxz)
        if 1 in which:
            syz = at(s + SYZ, i, c)
            syy, szz = at(s + SYY, i, c), at(s + SZZ, i, c)
            down_sxy = sxy - at(s + SXY, i - 1, c)
            down_sxz = sxz - at(s + SXZ, i - 1, c)
            out[1] = down_sxy + up_y(s + SYY, i, c, syy) + down_z(syz)
            out[2] = down_sxz + down_y(s + SYZ, i, c, syz) + up_z(szz)
        return out

    def velocity_plane(i, which, slot=None, fresh=False):
        for c in range(chunks):
            buoyancy = mats[0, i, rows_of(c), :]
            both = [force(s, i, c, which) for s in (0, 9)]
            old = [[at(s + d, i, c) for d in range(3)] for s in (0, 9)]
            for d in which:
                for n, s in enumerate((0, 9)):
                    state[s + d, i, rows_of(c), :] = old[n][d] + buoyancy * both[n][d]
            if slot is not None:
                term = both[0][0] * old[1][0] + both[0][1] * old[1][1] + both[0][2] * old[1][2]
                if not fresh:
                    term = acc[0, slot, rows_of(c), :] + term
                acc[0, slot, rows_of(c), :] = term

    def strain(s, i, c):
        vx, vy, vz = at(s + VX, i, c), at(s + VY, i, c), at(s + VZ, i, c)
        return [
            vx - at(s + VX, i - 1, c),
            down_y(s + VY, i, c, vy),
            down_z(vz),
            up_z(vy) + up_y(s + VZ, i, c, vz),
            up_z(vx) + (at(s + VZ, i + 1, c) - vz),
            up_y(s + VX, i, c, vx) + (at(s + VY, i + 1, c) - vy),
        ]

    def stress_chunk(i, c, step, slot=None, fresh=False, final=False, rim=None):
        m = [None] + [mats[k, i, rows_of(c), :] for k in range(1, 10)]
        both = []
        for s in (0, 9):
            e = strain(s, i, c)
            both.append(e)
            if s == 0:
                inject = wavelet[step] * image[i, rows_of(c), :]
            elif rim is None:
                inject = data[step - start, i - DEPTH, rows_of(c), :]
            else:
                inject = at(*RIM[rim][step // DEPTH], c)
            rates = [
                m[1] * e[0] + m[2] * e[1] + m[3] * e[2],
                m[2] * e[0] + m[4] * e[1] + m[5] * e[2],
                m[3] * e[0] + m[5] * e[1] + m[6] * e[2] + inject,
                m[7] * e[3],
                m[8] * e[4],
                m[9] * e[5],
            ]
            for f, rate in enumerate(rates):
                state[s + SXX + f, i, rows_of(c), :] = at(s + SXX + f, i, c) + rate
        if slot is None:
            return
        f, a = both
        terms = [
            f[0] * a[0],
            f[0] * a[1] + f[1] * a[0],
            f[0] * a[2] + f[2] * a[0],
            f[1] * a[1],
            f[1] * a[2] + f[2] * a[1],
            f[2] * a[2],
            f[3] * a[3],
            f[4] * a[4],
            f[5] * a[5],
        ]
        for n, term in enumerate(terms):
            if not fresh:
                term = acc[1 + n, slot, rows_of(c), :] + term
            if final:
                rows_ref[c, pl.ds((1 + n) * OWN + slot, 8, stride=10 * OWN), :] = scale * term
            else:
                acc[1 + n, slot, rows_of(c), :] = term
        if final:
            rows_ref[c, pl.ds(slot, 8, stride=10 * OWN), :] = scale * acc[0, slot, rows_of(c), :]

    inner, low, high = DEPTH + OWN, DEPTH - 1, DEPTH + OWN
    for at_step in range(DEPTH):
        step = at_step if first else DEPTH + at_step
        fresh = first and at_step == 0
        final = not first and at_step == DEPTH - 1
        velocity_plane(at_step, (0,))
        if at_step == 0:
            velocity_plane(low, (0, 1, 2))

        def velocity_own(x, carry):
            velocity_plane(DEPTH + x, (0, 1, 2), x, fresh)
            return carry

        lax.fori_loop(0, OWN, velocity_own, 0)
        if at_step == 0:
            velocity_plane(high, (0, 1, 2))
        velocity_plane(LENGTH - 1 - at_step, (1, 2))
        if at_step == 0:
            data_copy.wait()
            for c in range(chunks):
                stress_chunk(low, c, step, rim=0)
                stress_chunk(high, c, step, rim=1)
        if not final:

            def stress_own(x, carry):
                for c in range(chunks):
                    stress_chunk(DEPTH + x, c, step, x, fresh)
                return carry

            lax.fori_loop(0, OWN, stress_own, 0)
            continue
        copies = []
        for c in range(chunks):

            def stress_last(x, carry):
                for n in range(4):
                    stress_chunk(DEPTH + 4 * x + n, c, step, 4 * x + n, fresh, True)
                return carry

            lax.fori_loop(0, OWN // 4, stress_last, 0)
            copy = pltpu.make_async_copy(rows_ref.at[c], packed.at[c], sems.at[c])
            copy.start()
            copies.append(copy)
        for copy in copies:
            copy.wait()

    if first:
        fill_payloads(False, state, cross, chip)


def in_vmem(x):
    return pltpu.with_memory_space_constraint(x, VMEM)


def in_hbm(x):
    return pltpu.with_memory_space_constraint(x, pltpu.HBM)


WHOLE = pl.BlockSpec(memory_space=VMEM)
SCALARS = pl.BlockSpec(memory_space=pltpu.SMEM)
IN_HBM = pl.BlockSpec(memory_space=pltpu.HBM)


def estimate(flops, moved):
    return pl.CostEstimate(flops=flops, bytes_accessed=moved, transcendentals=0)


def run_phase(first, scalars, state, middle, data):
    y_rows, z_rows = state.shape[2:]
    chunks = y_rows // 8
    outs = [VMEM(state.shape, jnp.float32), VMEM((10, OWN, y_rows, z_rows), jnp.float32)]
    specs = [SCALARS] * len(scalars) + [WHOLE]
    aliases = {len(scalars): 0}
    if first:
        (gathered,) = middle
        middle = [in_hbm(gathered.reshape(chunks, 8 * ROWS, z_rows))]
        specs += [IN_HBM]
        outs += [VMEM((10, LENGTH, y_rows, z_rows), jnp.float32), VMEM((LENGTH, y_rows, z_rows), jnp.float32)]
        outs += [VMEM((sizes(False)[2], y_rows, z_rows), jnp.float32)] * 2
        out_specs = [WHOLE] * len(outs)
        rows = VMEM((chunks, 8 * ROWS, z_rows), jnp.float32)
    else:
        middle = [in_vmem(x) for x in middle]
        specs += [WHOLE] * len(middle)
        aliases[len(scalars) + 1] = 1
        outs.append(pltpu.HBM((chunks, 8 * 10 * OWN, z_rows), jnp.float32))
        out_specs = [WHOLE, WHOLE, IN_HBM]
        rows = VMEM((chunks, 8 * 10 * OWN, z_rows), jnp.float32)
    cells = (OWN + 2) * y_rows * z_rows * DEPTH
    return pl.pallas_call(
        functools.partial(phase_kernel, first, y_rows, z_rows),
        out_shape=tuple(outs),
        in_specs=specs + [IN_HBM],
        out_specs=tuple(out_specs),
        scratch_shapes=[
            rows,
            VMEM((DEPTH, OWN, y_rows, z_rows), jnp.float32),
            pltpu.SemaphoreType.DMA((chunks + 1,)),
        ],
        input_output_aliases=aliases,
        cost_estimate=estimate(160 * cells, 100 * cells),
        compiler_params=pltpu.CompilerParams(vmem_limit_bytes=6 << 20),
        name="phase_first" if first else "phase_last",
    )(*scalars, in_vmem(state), *middle, in_hbm(data))


def swap_across(value):
    peers = lax.axis_size("slab")
    return lax.ppermute(value, "slab", [p for i in range(1, peers - 1, 2) for p in ((i, i + 1), (i + 1, i))])


def swap_on_chip(value):
    peers = lax.axis_size("slab")
    return lax.ppermute(value, "slab", [p for i in range(0, peers, 2) for p in ((i, i + 1), (i + 1, i))])


def body(
    forward_state,
    adjoint_state,
    materials,
    wavelet,
    encoding,
    source_cells,
    receiver_depth,
    receiver_data,
):
    _, comps, own, y_rows, z_rows = forward_state.shape
    shots = lax.axis_size("shot")
    small = pltpu.CompilerParams(vmem_limit_bytes=2 << 20)

    own_rows, far, near = pl.pallas_call(
        edges_kernel,
        out_shape=(
            VMEM((10 * own, z_rows), jnp.float32),
            VMEM((10 * DEPTH, z_rows), jnp.float32),
            VMEM((10 * DEPTH, z_rows), jnp.float32),
        ),
        in_specs=[IN_HBM],
        out_specs=(WHOLE,) * 3,
        scratch_shapes=[pltpu.SemaphoreType.DMA],
        compiler_params=small,
        name="edges",
    )(in_hbm(materials.reshape(10 * own, z_rows)))
    far, near = swap_across(far), swap_on_chip(near)
    copies = pl.pallas_call(
        spread_kernel,
        out_shape=pltpu.HBM((shots, ROWS, z_rows), jnp.float32),
        in_specs=[WHOLE] * 3,
        out_specs=IN_HBM,
        scratch_shapes=[VMEM((ROWS, z_rows), jnp.float32), pltpu.SemaphoreType.DMA((shots,))],
        cost_estimate=estimate(1000, 4 * shots * ROWS * z_rows),
        compiler_params=small,
        name="spread",
    )(in_vmem(own_rows), in_vmem(far), in_vmem(near))
    gathered = lax.all_to_all(copies, "shot", split_axis=0, concat_axis=0, tiled=True)

    z_at = lax.broadcasted_iota(jnp.int32, (own, y_rows, z_rows), 2)
    probe = z_at == receiver_depth[:, :, None]
    data = jnp.where(probe[None], receiver_data[0][:, :, :, None], 0.0)

    payload = VMEM((sizes(True)[2] + STEPS // DEPTH, y_rows, z_rows), jnp.float32)
    whole_state = VMEM((2 * comps, LENGTH, y_rows, z_rows), jnp.float32)
    moved = 8 * comps * own * y_rows * z_rows
    state, cross, chip = pl.pallas_call(
        stage_kernel,
        out_shape=(whole_state, payload, payload),
        in_specs=[IN_HBM, IN_HBM, WHOLE],
        out_specs=(WHOLE,) * 3,
        scratch_shapes=[pltpu.SemaphoreType.DMA((2 * comps,))],
        cost_estimate=estimate(1000, moved),
        compiler_params=small,
        name="stage",
    )(in_hbm(forward_state[0]), in_hbm(adjoint_state[0]), in_vmem(data))
    cross, chip = swap_across(cross), swap_on_chip(chip)
    state = pl.pallas_call(
        join_kernel,
        out_shape=whole_state,
        in_specs=[WHOLE] * 3,
        out_specs=WHOLE,
        input_output_aliases={0: 0},
        cost_estimate=estimate(1000, moved),
        compiler_params=small,
        name="join",
    )(in_vmem(state), in_vmem(cross), in_vmem(chip))

    outs = run_phase(True, (wavelet, encoding, source_cells), state, [gathered], data)
    state, acc, mats, image, cross, chip = outs
    cross, chip = swap_across(cross), swap_on_chip(chip)
    outs = run_phase(False, (wavelet,), state, [acc, cross, chip, mats, image], data)
    state, _, packed = outs

    tiles = lax.all_to_all(packed.reshape(y_rows, 10 * own, z_rows), "shot", 0, 0, tiled=True)
    gradient = jnp.sum(tiles, axis=0).reshape(10, own, 1, z_rows)
    forward_out = state[None, :comps, DEPTH : DEPTH + own]
    adjoint_out = state[None, comps:, DEPTH : DEPTH + own]
    return forward_out, adjoint_out, gradient


def solution(mesh):
    state_spec = P("shot", None, "slab", None, None)
    return jax.shard_map(
        body,
        mesh=mesh,
        in_specs=(
            state_spec,
            state_spec,
            P(None, "slab", "shot", None),
            P(),
            P("shot", None),
            P("shot", None),
            P("slab", None),
            P("shot", None, "slab", None),
        ),
        out_specs=(state_spec, state_spec, P(None, "slab", "shot", None)),
        check_vma=False,
    )
```

```python
import functools

import jax
import jax.numpy as jnp
from jax import lax
from jax.experimental import pallas as pl
from jax.experimental.pallas import tpu as pltpu
from jax.sharding import PartitionSpec as P

STEPS = 4
DEPTH = 2
OWN = 8
LENGTH = OWN + 2 * DEPTH
VX, VY, VZ, SXX, SYY, SZZ, SYZ, SXZ, SXY = range(9)
step_size = 0.25
VMEM = pltpu.VMEM
ROWS = 10 * OWN
RIM_ROWS = DEPTH + 9

BOTH = (SXX, SXY, SXZ)
UP = [(VX, OWN - 2), (VY, OWN - 1), (VZ, OWN - 1)]
UP += [(f, OWN - 2) for f in BOTH] + [(f, OWN - 1) for f in range(SXX, SXY + 1)]
DOWN = [(VX, 0), (VY, 1), (VZ, 1)] + [(f, j) for f in range(SXX, SXY + 1) for j in (0, 1)]
UP_FIRST = UP + [(VX, OWN - 1)]
DOWN_FIRST = DOWN + [(VY, 0), (VZ, 0)]


def sizes(first):
    up, down = (UP_FIRST, DOWN_FIRST) if first else (UP, DOWN)
    return up, down, 2 * max(len(up), len(down))


def is_odd():
    return lax.rem(lax.axis_index("slab"), 2) == 1


def fill_payloads(first, state, cross, chip, data=None):
    up, down, base = sizes(first)

    def fill(target, planes, layer):
        for s in range(2):
            for n, (f, j) in enumerate(planes):
                target[s * len(planes) + n] = state[9 * s + f, DEPTH + j]
        if data is not None:
            for n in range(STEPS // DEPTH):
                target[base + n] = data[n * DEPTH, layer]

    @pl.when(is_odd())
    def _():
        fill(cross, up, OWN - 1)
        fill(chip, down, 0)

    @pl.when(jnp.logical_not(is_odd()))
    def _():
        fill(cross, down, 0)
        fill(chip, up, OWN - 1)


RIM = (((VY, 0), (VZ, 0)), ((VX, LENGTH - 1), (9 + VX, LENGTH - 1)))


def drain_payloads(first, state, cross, chip):
    up, down, base = sizes(first)

    def drain(source, planes, shift, at):
        for s in range(2):
            for n, (f, j) in enumerate(planes):
                state[9 * s + f, DEPTH + j + shift] = source[s * len(planes) + n]
        if first:
            for n, place in enumerate(RIM[at]):
                state[place] = source[base + n]

    @pl.when(is_odd())
    def _():
        drain(chip, up, -OWN, 0)
        drain(cross, down, OWN, 1)

    @pl.when(jnp.logical_not(is_odd()))
    def _():
        drain(cross, up, -OWN, 0)
        drain(chip, down, OWN, 1)


def spread_kernel(materials, out, block, sem, sems):
    copy = pltpu.make_async_copy(materials, block, sem)
    copy.start()
    copy.wait()
    copies = [pltpu.make_async_copy(block, out.at[j], sems.at[j]) for j in range(out.shape[0])]
    for copy in copies:
        copy.start()
    for copy in copies:
        copy.wait()


def turn_kernel(gathered, mats, cross, chip, rows_ref, sems):
    chunks = gathered.shape[0]
    copies = [pltpu.make_async_copy(gathered.at[c], rows_ref.at[c], sems.at[c]) for c in range(chunks)]
    for copy in copies:
        copy.start()
    for c in range(chunks):
        copies[c].wait()
        for r in range(ROWS):
            plane = step_size * rows_ref[c, pl.ds(r, 8, stride=ROWS), :]
            mats[r // OWN, DEPTH + r % OWN, pl.ds(8 * c, 8), :] = plane

    def fill(target, layers):
        for n, (m, j) in enumerate(rim_planes(layers)):
            target[n] = mats[m, DEPTH + j]

    @pl.when(is_odd())
    def _():
        fill(cross, (OWN - 2, OWN - 1, OWN - 1))
        fill(chip, (0, 1, 0))

    @pl.when(jnp.logical_not(is_odd()))
    def _():
        fill(cross, (0, 1, 0))
        fill(chip, (OWN - 2, OWN - 1, OWN - 1))


def rim_planes(layers):
    return [(0, layers[0]), (0, layers[1])] + [(m, layers[2]) for m in range(1, 10)]


def drain_rims(mats, cross, chip):
    def drain(source, layers):
        for n, (m, j) in enumerate(rim_planes(layers)):
            mats[m, DEPTH + j] = source[n]

    below, above = (-2, -1, -1), (OWN, OWN + 1, OWN)

    @pl.when(is_odd())
    def _():
        drain(chip, below)
        drain(cross, above)

    @pl.when(jnp.logical_not(is_odd()))
    def _():
        drain(cross, below)
        drain(chip, above)


def stage_kernel(forward, adjoint, data, state, cross, chip, sems):
    inner = pl.ds(DEPTH, OWN)
    copies = [
        pltpu.make_async_copy(part.at[f], state.at[9 * s + f, inner], sems.at[9 * s + f])
        for s, part in enumerate((forward, adjoint))
        for f in range(9)
    ]
    for copy in copies:
        copy.start()
    for copy in copies:
        copy.wait()
    fill_payloads(True, state, cross, chip, data)


def join_kernel(state_in, cross, chip, state):
    drain_payloads(True, state, cross, chip)


def draw_image(encoding, cells, image):
    layers, y_rows, z_rows = image.shape
    image[...] = jnp.zeros(image.shape, jnp.float32)
    lane = lax.broadcasted_iota(jnp.int32, (1, z_rows), 1)
    first_x = lax.axis_index("slab") * OWN - DEPTH
    for n in range(cells.shape[1]):
        cell = cells[0, n]
        x = cell // (y_rows * z_rows) - first_x
        inside = jnp.logical_and(x >= 0, x < layers)
        x = jnp.where(inside, x, 0)
        y = lax.rem(cell // z_rows, y_rows)
        sign = jnp.where(inside, 2 * encoding[0, n] - 1, 0).astype(jnp.float32)
        spot = jnp.where(lane == lax.rem(cell, z_rows), sign, 0.0)
        image[x, pl.ds(y, 1), :] = image[x, pl.ds(y, 1), :] + spot


def phase_kernel(part, y_rows, z_rows, *refs):
    first = part != "last"
    if part == "early":
        wavelet, encoding, cells, _, mats, data_in, state, acc, image, data, sems = refs
    elif part == "rest":
        wavelet, _, _, _, cross_in, chip_in, image, data_in, state, acc, mats, cross, chip, data, sems = refs
    else:
        wavelet, _, _, cross_in, chip_in, mats, image, data_in, state, acc, packed, data, rows_ref, sems = refs

    chunks = y_rows // 8
    scale = float(y_rows * STEPS) ** (-0.5)
    row = lax.broadcasted_iota(jnp.int32, (8, z_rows), 0)
    lane = lax.broadcasted_iota(jnp.int32, (8, z_rows), 1)
    row_first, row_last = row == 0, row == 7
    lane_first, lane_last = lane == 0, lane == z_rows - 1
    nought = jnp.zeros((8, z_rows), jnp.float32)

    start = 0 if first else DEPTH
    data_copy = pltpu.make_async_copy(data_in.at[pl.ds(start, DEPTH)], data, sems.at[0])
    data_copy.start()
    if part == "early":
        draw_image(encoding, cells, image)
    elif part == "rest":
        drain_rims(mats, cross_in, chip_in)
    else:
        drain_payloads(False, state, cross_in, chip_in)

    def rows_of(c):
        return pl.ds(8 * c, 8)

    def at(f, i, c):
        return state[f, i, rows_of(c), :]

    def up_y(f, i, c, a):
        b = at(f, i, c + 1) if c + 1 < chunks else nought
        return pltpu.roll(jnp.where(row_first, b, a), 7, 0) - a

    def down_y(f, i, c, a):
        b = at(f, i, c - 1) if c > 0 else nought
        return a - pltpu.roll(jnp.where(row_last, b, a), 1, 0)

    def up_z(a):
        return pltpu.roll(jnp.where(lane_first, 0.0, a), z_rows - 1, 1) - a

    def down_z(a):
        return a - pltpu.roll(jnp.where(lane_last, 0.0, a), 1, 1)

    def force(s, i, c, which):
        sxy, sxz = at(s + SXY, i, c), at(s + SXZ, i, c)
        out = [None] * 3
        if 0 in which:
            up_x = at(s + SXX, i + 1, c) - at(s + SXX, i, c)
            out[0] = up_x + down_y(s + SXY, i, c, sxy) + down_z(sxz)
        if 1 in which:
            syz = at(s + SYZ, i, c)
            syy, szz = at(s + SYY, i, c), at(s + SZZ, i, c)
            down_sxy = sxy - at(s + SXY, i - 1, c)
            down_sxz = sxz - at(s + SXZ, i - 1, c)
            out[1] = down_sxy + up_y(s + SYY, i, c, syy) + down_z(syz)
            out[2] = down_sxz + down_y(s + SYZ, i, c, syz) + up_z(szz)
        return out

    def velocity_plane(i, which, slot=None, fresh=False):
        for c in range(chunks):
            buoyancy = mats[0, i, rows_of(c), :]
            both = [force(s, i, c, which) for s in (0, 9)]
            old = [[at(s + d, i, c) for d in range(3)] for s in (0, 9)]
            for d in which:
                for n, s in enumerate((0, 9)):
                    state[s + d, i, rows_of(c), :] = old[n][d] + buoyancy * both[n][d]
            if slot is not None:
                term = both[0][0] * old[1][0] + both[0][1] * old[1][1] + both[0][2] * old[1][2]
                if not fresh:
                    term = acc[0, slot, rows_of(c), :] + term
                acc[0, slot, rows_of(c), :] = term

    def strain(s, i, c):
        vx, vy, vz = at(s + VX, i, c), at(s + VY, i, c), at(s + VZ, i, c)
        return [
            vx - at(s + VX, i - 1, c),
            down_y(s + VY, i, c, vy),
            down_z(vz),
            up_z(vy) + up_y(s + VZ, i, c, vz),
            up_z(vx) + (at(s + VZ, i + 1, c) - vz),
            up_y(s + VX, i, c, vx) + (at(s + VY, i + 1, c) - vy),
        ]

    def stress_chunk(i, c, step, slot=None, fresh=False, final=False, rim=None):
        m = [None] + [mats[k, i, rows_of(c), :] for k in range(1, 10)]
        both = []
        for s in (0, 9):
            e = strain(s, i, c)
            both.append(e)
            if s == 0:
                inject = wavelet[step] * image[i, rows_of(c), :]
            elif rim is None:
                inject = data[step - start, i - DEPTH, rows_of(c), :]
            else:
                inject = at(*RIM[rim][step // DEPTH], c)
            rates = [
                m[1] * e[0] + m[2] * e[1] + m[3] * e[2],
                m[2] * e[0] + m[4] * e[1] + m[5] * e[2],
                m[3] * e[0] + m[5] * e[1] + m[6] * e[2] + inject,
                m[7] * e[3],
                m[8] * e[4],
                m[9] * e[5],
            ]
            for f, rate in enumerate(rates):
                state[s + SXX + f, i, rows_of(c), :] = at(s + SXX + f, i, c) + rate
        if slot is None:
            return
        f, a = both
        terms = [
            f[0] * a[0],
            f[0] * a[1] + f[1] * a[0],
            f[0] * a[2] + f[2] * a[0],
            f[1] * a[1],
            f[1] * a[2] + f[2] * a[1],
            f[2] * a[2],
            f[3] * a[3],
            f[4] * a[4],
            f[5] * a[5],
        ]
        for n, term in enumerate(terms):
            if not fresh:
                term = acc[1 + n, slot, rows_of(c), :] + term
            if final:
                rows_ref[pl.ds(10 * slot + 1 + n + 8 * c * ROWS, 8, stride=ROWS), :] = scale * term
            else:
                acc[1 + n, slot, rows_of(c), :] = term
        if final:
            term = scale * acc[0, slot, rows_of(c), :]
            rows_ref[pl.ds(10 * slot + 8 * c * ROWS, 8, stride=ROWS), :] = term

    low, high = DEPTH - 1, DEPTH + OWN

    def velocity_own(fresh):
        def one(x, carry):
            velocity_plane(DEPTH + x, (0, 1, 2), x, fresh)
            return carry

        lax.fori_loop(0, OWN, one, 0)

    def stress_own(step, begin, end, fresh=False, final=False):
        def one(x, carry):
            for c in range(chunks):
                stress_chunk(DEPTH + x, c, step, x, fresh, final)
            return carry

        lax.fori_loop(begin, end, one, 0)

    def velocity_rims(at_step):
        velocity_plane(at_step, (0,))
        if at_step == 0:
            velocity_plane(low, (0, 1, 2))
            velocity_plane(high, (0, 1, 2))
        velocity_plane(LENGTH - 1 - at_step, (1, 2))

    def stress_rims(step):
        for c in range(chunks):
            stress_chunk(low, c, step, rim=0)
            stress_chunk(high, c, step, rim=1)

    if part == "early":
        velocity_own(True)
        data_copy.wait()
        stress_own(0, 1, OWN - 1, True)
    elif part == "rest":
        velocity_rims(0)
        data_copy.wait()
        stress_rims(0)

        def ends(x, carry):
            slot = x * (OWN - 1)
            for c in range(chunks):
                stress_chunk(DEPTH + slot, c, 0, slot, True)
            return carry

        lax.fori_loop(0, 2, ends, 0)
        velocity_own(False)
        velocity_rims(1)
        stress_own(1, 0, OWN)
        fill_payloads(False, state, cross, chip)
    else:
        velocity_own(False)
        velocity_rims(0)
        data_copy.wait()
        stress_rims(DEPTH)
        stress_own(DEPTH, 0, OWN)
        velocity_own(False)
        velocity_rims(1)
        copies = []
        for n in range(2):
            stress_own(DEPTH + 1, n * OWN // 2, (n + 1) * OWN // 2, False, True)
            half = pl.ds(n * ROWS // 2, ROWS // 2)
            whole = rows_ref.reshape(y_rows, ROWS, z_rows)
            copies.append(pltpu.make_async_copy(whole.at[:, half], packed.at[:, half], sems.at[1 + n]))
            copies[-1].start()
        for copy in copies:
            copy.wait()


def sum_kernel(tiles, out, rows_ref, total, sems):
    parts = tiles.shape[0] // 8
    copies = [
        pltpu.make_async_copy(tiles.at[pl.ds(8 * n, 8)], rows_ref.at[pl.ds(8 * n, 8)], sems.at[n])
        for n in range(parts)
    ]
    for copy in copies:
        copy.start()
    for n in range(parts):
        copies[n].wait()
        for g in range(ROWS // 8):
            rows = pl.ds(8 * g, 8)
            values = [rows_ref[8 * n + j, rows, :] for j in range(8)]
            while len(values) > 1:
                values = [a + b for a, b in zip(values[::2], values[1::2])]
            total[rows, :] = values[0] if n == 0 else total[rows, :] + values[0]
    for m in range(10):
        out[pl.ds(OWN * m, OWN), :] = total[pl.ds(m, OWN, stride=10), :]


def in_vmem(x):
    return pltpu.with_memory_space_constraint(x, VMEM)


def in_hbm(x):
    return pltpu.with_memory_space_constraint(x, pltpu.HBM)


WHOLE = pl.BlockSpec(memory_space=VMEM)
SCALARS = pl.BlockSpec(memory_space=pltpu.SMEM)
IN_HBM = pl.BlockSpec(memory_space=pltpu.HBM)


def estimate(flops, moved):
    return pl.CostEstimate(flops=flops, bytes_accessed=moved, transcendentals=0)


def run_phase(part, scalars, state, middle, data):
    y_rows, z_rows = state.shape[2:]
    count = len(scalars)
    outs = [VMEM(state.shape, jnp.float32), VMEM((10, OWN, y_rows, z_rows), jnp.float32)]
    aliases = {count: 0}
    scratch = [VMEM((DEPTH, OWN, y_rows, z_rows), jnp.float32)]
    payload = VMEM((sizes(False)[2], y_rows, z_rows), jnp.float32)
    out_specs = [WHOLE, WHOLE]
    if part == "early":
        outs += [VMEM((LENGTH, y_rows, z_rows), jnp.float32)]
        out_specs += [WHOLE]
    elif part == "rest":
        outs += [VMEM((10, LENGTH, y_rows, z_rows), jnp.float32), payload, payload]
        aliases.update({count + 1: 1, count + 2: 2})
        out_specs += [WHOLE] * 3
    else:
        outs += [pltpu.HBM((y_rows, ROWS, z_rows), jnp.float32)]
        aliases.update({count + 1: 1})
        scratch += [VMEM((y_rows * ROWS, z_rows), jnp.float32)]
        out_specs += [IN_HBM]
    cells = (OWN + 2) * y_rows * z_rows * (2 if part == "last" else 1)
    return pl.pallas_call(
        functools.partial(phase_kernel, part, y_rows, z_rows),
        out_shape=tuple(outs),
        in_specs=[SCALARS] * count + [WHOLE] * (1 + len(middle)) + [IN_HBM],
        out_specs=tuple(out_specs),
        scratch_shapes=scratch + [pltpu.SemaphoreType.DMA((3,))],
        input_output_aliases=aliases,
        cost_estimate=estimate(160 * cells, 100 * cells),
        compiler_params=pltpu.CompilerParams(vmem_limit_bytes=4 << 20),
        name="steps_" + part,
    )(*scalars, in_vmem(state), *[in_vmem(x) for x in middle], in_hbm(data))


def swap_across(value):
    peers = lax.axis_size("slab")
    return lax.ppermute(value, "slab", [p for i in range(1, peers - 1, 2) for p in ((i, i + 1), (i + 1, i))])


def swap_on_chip(value):
    peers = lax.axis_size("slab")
    return lax.ppermute(value, "slab", [p for i in range(0, peers, 2) for p in ((i, i + 1), (i + 1, i))])


def body(
    forward_state,
    adjoint_state,
    materials,
    wavelet,
    encoding,
    source_cells,
    receiver_depth,
    receiver_data,
):
    _, comps, own, y_rows, z_rows = forward_state.shape
    shots = lax.axis_size("shot")
    small = pltpu.CompilerParams(vmem_limit_bytes=2 << 20)

    copies = pl.pallas_call(
        spread_kernel,
        out_shape=pltpu.HBM((shots, ROWS, z_rows), jnp.float32),
        in_specs=[IN_HBM],
        out_specs=IN_HBM,
        scratch_shapes=[
            VMEM((ROWS, z_rows), jnp.float32),
            pltpu.SemaphoreType.DMA,
            pltpu.SemaphoreType.DMA((shots,)),
        ],
        cost_estimate=estimate(1000, 4 * shots * ROWS * z_rows),
        compiler_params=small,
        name="spread",
    )(in_hbm(materials.reshape(ROWS, z_rows)))
    gathered = lax.all_to_all(copies, "shot", split_axis=0, concat_axis=0, tiled=True)

    z_at = lax.broadcasted_iota(jnp.int32, (own, y_rows, z_rows), 2)
    probe = z_at == receiver_depth[:, :, None]
    data = jnp.where(probe[None], receiver_data[0][:, :, :, None], 0.0)

    payload = VMEM((sizes(True)[2] + STEPS // DEPTH, y_rows, z_rows), jnp.float32)
    whole_state = VMEM((2 * comps, LENGTH, y_rows, z_rows), jnp.float32)
    moved = 8 * comps * own * y_rows * z_rows
    state, cross, chip = pl.pallas_call(
        stage_kernel,
        out_shape=(whole_state, payload, payload),
        in_specs=[IN_HBM, IN_HBM, WHOLE],
        out_specs=(WHOLE,) * 3,
        scratch_shapes=[pltpu.SemaphoreType.DMA((2 * comps,))],
        cost_estimate=estimate(1000, moved),
        compiler_params=small,
        name="stage",
    )(in_hbm(forward_state[0]), in_hbm(adjoint_state[0]), in_vmem(data))
    cross, chip = swap_across(cross), swap_on_chip(chip)
    state = pl.pallas_call(
        join_kernel,
        out_shape=whole_state,
        in_specs=[WHOLE] * 3,
        out_specs=WHOLE,
        input_output_aliases={0: 0},
        cost_estimate=estimate(1000, moved),
        compiler_params=small,
        name="join",
    )(in_vmem(state), in_vmem(cross), in_vmem(chip))

    chunks = y_rows // 8
    rim = VMEM((RIM_ROWS, y_rows, z_rows), jnp.float32)
    mats, far, near = pl.pallas_call(
        turn_kernel,
        out_shape=(VMEM((10, LENGTH, y_rows, z_rows), jnp.float32), rim, rim),
        in_specs=[IN_HBM],
        out_specs=(WHOLE,) * 3,
        scratch_shapes=[
            VMEM((chunks, 8 * ROWS, z_rows), jnp.float32),
            pltpu.SemaphoreType.DMA((chunks,)),
        ],
        cost_estimate=estimate(1000, 8 * shots * ROWS * z_rows),
        compiler_params=pltpu.CompilerParams(vmem_limit_bytes=4 << 20),
        name="turn",
    )(in_hbm(gathered.reshape(chunks, 8 * ROWS, z_rows)))
    far, near = swap_across(far), swap_on_chip(near)
    state, acc, image = run_phase("early", (wavelet, encoding, source_cells), state, [mats], data)
    outs = run_phase("rest", (wavelet,), state, [acc, mats, far, near, image], data)
    state, acc, mats, cross, chip = outs
    cross, chip = swap_across(cross), swap_on_chip(chip)
    state, _, packed = run_phase("last", (wavelet,), state, [acc, cross, chip, mats, image], data)

    tiles = lax.all_to_all(packed, "shot", 0, 0, tiled=True)
    gradient = pl.pallas_call(
        sum_kernel,
        out_shape=jax.ShapeDtypeStruct((ROWS, z_rows), jnp.float32),
        in_specs=[IN_HBM],
        out_specs=WHOLE,
        scratch_shapes=[
            VMEM((shots, ROWS, z_rows), jnp.float32),
            VMEM((ROWS, z_rows), jnp.float32),
            pltpu.SemaphoreType.DMA((shots // 8,)),
        ],
        cost_estimate=estimate(shots * ROWS * z_rows, 4 * shots * ROWS * z_rows),
        compiler_params=pltpu.CompilerParams(vmem_limit_bytes=4 << 20),
        name="sum",
    )(in_hbm(tiles))
    gradient = gradient.reshape(10, own, 1, z_rows)
    forward_out = state[None, :comps, DEPTH : DEPTH + own]
    adjoint_out = state[None, comps:, DEPTH : DEPTH + own]
    return forward_out, adjoint_out, gradient


def solution(mesh):
    state_spec = P("shot", None, "slab", None, None)
    return jax.shard_map(
        body,
        mesh=mesh,
        in_specs=(
            state_spec,
            state_spec,
            P(None, "slab", "shot", None),
            P(),
            P("shot", None),
            P("shot", None),
            P("slab", None),
            P("shot", None, "slab", None),
        ),
        out_specs=(state_spec, state_spec, P(None, "slab", "shot", None)),
        check_vma=False,
    )
```

```python
import functools

import jax
import jax.numpy as jnp
from jax import lax
from jax.experimental import pallas as pl
from jax.experimental.pallas import tpu as pltpu
from jax.sharding import PartitionSpec as P

STEPS = 4
DEPTH = STEPS
OWN = 8
LENGTH = OWN + 2 * DEPTH
VX, VY, VZ, SXX, SYY, SZZ, SYZ, SXZ, SXY = range(9)
step_size = 0.25
VMEM = pltpu.VMEM
ROWS = 10 * OWN

UP = [(f, OWN - n, n) for f, n in enumerate((4, 3, 3, 4, 3, 3, 3, 4, 4))]
DOWN = [(f, 0, n) for f, n in enumerate((3, 4, 4, 4, 4, 4, 4, 4, 4))]
RIM_SLOTS = [(t, k) for t in range(STEPS - 1) for k in range(DEPTH - 1 - t)]
RIM_BASE = [0, 3, 5]
RECEIVER_CELLS = 4
PAYLOAD = 2 * sum(n for _, _, n in DOWN) + 1
HALO_COPIES = 4 * len(UP) + 2
RIM_PLANES = DEPTH + 9 * (DEPTH - 1)


def is_odd():
    return lax.rem(lax.axis_index("slab"), 2) == 1


def pieces(planes):
    place, out = 0, []
    for s in range(2):
        for f, first, n in planes:
            out.append((9 * s + f, first, n, place))
            place += n
    return out


def by_parity(odd, even):
    pl.when(is_odd())(odd)
    pl.when(jnp.logical_not(is_odd()))(even)


def spread_kernel(materials, out, block, sem, sems):
    copy = pltpu.make_async_copy(materials, block, sem)
    copy.start()
    copy.wait()
    copies = [pltpu.make_async_copy(block, out.at[j], sems.at[j]) for j in range(out.shape[0])]
    for copy in copies:
        copy.start()
    for copy in copies:
        copy.wait()


def turn_kernel(gathered, forward, adjoint, mats, cross, chip, state, rows_ref, sems):
    chunks = gathered.shape[0]
    copies = [pltpu.make_async_copy(gathered.at[c], rows_ref.at[c], sems.at[c]) for c in range(chunks)]
    for copy in copies:
        copy.start()
    for c in range(chunks):
        copies[c].wait()
        for r in range(ROWS):
            plane = step_size * rows_ref[c, pl.ds(r, 8, stride=ROWS), :]
            mats[r // OWN, DEPTH + r % OWN, pl.ds(8 * c, 8), :] = plane

    copies = [
        pltpu.make_async_copy(part.at[f], state.at[9 * s + f, pl.ds(DEPTH, OWN)], sems.at[chunks + 9 * s + f])
        for s, part in enumerate((forward, adjoint))
        for f in range(9)
    ]
    for copy in copies:
        copy.start()

    def fill(target, upward):
        for n, (m, j) in enumerate(rim_planes()):
            target[n] = mats[m, DEPTH + (OWN - 1 - j if upward else j)]

    def odd():
        fill(cross, True)
        fill(chip, False)

    def even():
        fill(cross, False)
        fill(chip, True)

    by_parity(odd, even)
    for copy in copies:
        copy.wait()


def rim_planes():
    return [(0, j) for j in range(DEPTH)] + [(m, j) for m in range(1, 10) for j in range(DEPTH - 1)]


def drain_rims(mats, cross, chip):
    def drain(source, below):
        for n, (m, j) in enumerate(rim_planes()):
            mats[m, DEPTH - 1 - j if below else DEPTH + OWN + j] = source[n]

    def odd():
        drain(chip, True)
        drain(cross, False)

    def even():
        drain(cross, True)
        drain(chip, False)

    by_parity(odd, even)


def stage_kernel(forward, adjoint, data, cross, chip, own, lines, sems):
    z_rows = data.shape[-1]
    fields = [
        pltpu.make_async_copy(part.at[f], own.at[9 * s + f], sems.at[9 * s + f])
        for s, part in enumerate((forward, adjoint))
        for f in range(9)
    ]
    for copy in fields:
        copy.start()
    for at, upward in enumerate((True, False)):
        line = jnp.zeros(data.shape[2:], jnp.float32)
        for n, (t, k) in enumerate(RIM_SLOTS):
            plane = data[t, OWN - 1 - k if upward else k]
            line = line + (pltpu.roll(plane, RECEIVER_CELLS * n, 1) if n else plane)
        lines[at] = line
    for copy in fields:
        copy.wait()

    def send(target, at, planes):
        copies = [(own.at[f, pl.ds(first, n)], target.at[pl.ds(place, n)]) for f, first, n, place in pieces(planes)]
        copies.append((lines.at[at], target.at[PAYLOAD - 1]))
        return copies

    def run(copies):
        copies = [pltpu.make_async_copy(a, b, sems.at[n]) for n, (a, b) in enumerate(copies)]
        for copy in copies:
            copy.start()
        for copy in copies:
            copy.wait()

    by_parity(
        lambda: run(send(cross, 0, UP) + send(chip, 1, DOWN)),
        lambda: run(send(cross, 1, DOWN) + send(chip, 0, UP)),
    )


def halo_copies(state, lines, below, above, sems):
    out = []
    for source, planes, shift, at in ((below, UP, DEPTH - OWN, 0), (above, DOWN, DEPTH + OWN, 1)):
        pairs = [
            (source.at[pl.ds(place, n)], state.at[f, pl.ds(first + shift, n)]) for f, first, n, place in pieces(planes)
        ]
        pairs.append((source.at[PAYLOAD - 1], lines.at[at]))
        for a, b in pairs:
            out.append(pltpu.make_async_copy(a, b, sems.at[len(out)]))
    return out


def draw_image(encoding, cells, image):
    layers, y_rows, z_rows = image.shape
    image[...] = jnp.zeros(image.shape, jnp.float32)
    lane = lax.broadcasted_iota(jnp.int32, (1, z_rows), 1)
    first_x = lax.axis_index("slab") * OWN - DEPTH
    for n in range(cells.shape[1]):
        cell = cells[0, n]
        x = cell // (y_rows * z_rows) - first_x
        inside = jnp.logical_and(x >= 0, x < layers)
        x = jnp.where(inside, x, 0)
        y = lax.rem(cell // z_rows, y_rows)
        sign = jnp.where(inside, 2 * encoding[0, n] - 1, 0).astype(jnp.float32)
        spot = jnp.where(lane == lax.rem(cell, z_rows), sign, 0.0)
        image[x, pl.ds(y, 1), :] = image[x, pl.ds(y, 1), :] + spot


def phase_kernel(part, y_rows, z_rows, *refs):
    if part == "early":
        wavelet, encoding, cells, _, mats, cross_in, chip_in, data_in, *refs = refs
        state, acc, image, rim_data, data, lines, sems = refs
    else:
        wavelet, _, _, _, cross_in, chip_in, image, rim_data, data, state, acc, mats, forward, adjoint, packed, rows_ref, final_state, sems = refs

    chunks = y_rows // 8
    scale = float(y_rows * STEPS) ** (-0.5)
    row = lax.broadcasted_iota(jnp.int32, (8, z_rows), 0)
    lane = lax.broadcasted_iota(jnp.int32, (8, z_rows), 1)
    row_first, row_last = row == 0, row == 7
    lane_first, lane_last = lane == 0, lane == z_rows - 1
    nought = jnp.zeros((8, z_rows), jnp.float32)

    def rows_of(c):
        return pl.ds(8 * c, 8)

    def at(f, i, c):
        return state[f, i, rows_of(c), :]

    def up_y(f, i, c, a):
        b = at(f, i, c + 1) if c + 1 < chunks else nought
        return pltpu.roll(jnp.where(row_first, b, a), 7, 0) - a

    def down_y(f, i, c, a):
        b = at(f, i, c - 1) if c > 0 else nought
        return a - pltpu.roll(jnp.where(row_last, b, a), 1, 0)

    def up_z(a):
        return pltpu.roll(jnp.where(lane_first, 0.0, a), z_rows - 1, 1) - a

    def down_z(a):
        return a - pltpu.roll(jnp.where(lane_last, 0.0, a), 1, 1)

    def force(s, i, c, which):
        sxy, sxz = at(s + SXY, i, c), at(s + SXZ, i, c)
        out = [None] * 3
        if 0 in which:
            up_x = at(s + SXX, i + 1, c) - at(s + SXX, i, c)
            out[0] = up_x + down_y(s + SXY, i, c, sxy) + down_z(sxz)
        if 1 in which:
            syz = at(s + SYZ, i, c)
            syy, szz = at(s + SYY, i, c), at(s + SZZ, i, c)
            down_sxy = sxy - at(s + SXY, i - 1, c)
            down_sxz = sxz - at(s + SXZ, i - 1, c)
            out[1] = down_sxy + up_y(s + SYY, i, c, syy) + down_z(syz)
            out[2] = down_sxz + down_y(s + SYZ, i, c, syz) + up_z(szz)
        return out

    def velocity_plane(i, which, slot=None, fresh=False, final=False):
        for c in range(chunks):
            buoyancy = mats[0, i, rows_of(c), :]
            both = [force(s, i, c, which) for s in (0, 9)]
            old = [[at(s + d, i, c) for d in range(3)] for s in (0, 9)]
            for d in which:
                for n, s in enumerate((0, 9)):
                    value = old[n][d] + buoyancy * both[n][d]
                    state[s + d, i, rows_of(c), :] = value
                    if final:
                        final_state[s + d, slot, rows_of(c), :] = value
            if slot is not None:
                term = both[0][0] * old[1][0] + both[0][1] * old[1][1] + both[0][2] * old[1][2]
                if not fresh:
                    term = acc[0, slot, rows_of(c), :] + term
                acc[0, slot, rows_of(c), :] = term

    def strain(s, i, c):
        vx, vy, vz = at(s + VX, i, c), at(s + VY, i, c), at(s + VZ, i, c)
        return [
            vx - at(s + VX, i - 1, c),
            down_y(s + VY, i, c, vy),
            down_z(vz),
            up_z(vy) + up_y(s + VZ, i, c, vz),
            up_z(vx) + (at(s + VZ, i + 1, c) - vz),
            up_y(s + VX, i, c, vx) + (at(s + VY, i + 1, c) - vy),
        ]

    def stress_chunk(i, c, step, slot=None, fresh=False, final=False, rim=None):
        m = [None] + [mats[k, i, rows_of(c), :] for k in range(1, 10)]
        both = []
        for s in (0, 9):
            e = strain(s, i, c)
            both.append(e)
            if s == 0:
                inject = wavelet[step] * image[i, rows_of(c), :]
            elif rim is None:
                inject = data[step, i - DEPTH, rows_of(c), :]
            else:
                inject = rim_data[rim[0], rim[1], rows_of(c), :]
            rates = [
                m[1] * e[0] + m[2] * e[1] + m[3] * e[2],
                m[2] * e[0] + m[4] * e[1] + m[5] * e[2],
                m[3] * e[0] + m[5] * e[1] + m[6] * e[2] + inject,
                m[7] * e[3],
                m[8] * e[4],
                m[9] * e[5],
            ]
            for f, rate in enumerate(rates):
                value = at(s + SXX + f, i, c) + rate
                if final:
                    final_state[s + SXX + f, slot, rows_of(c), :] = value
                else:
                    state[s + SXX + f, i, rows_of(c), :] = value
        if slot is None:
            return
        f, a = both
        terms = [
            f[0] * a[0],
            f[0] * a[1] + f[1] * a[0],
            f[0] * a[2] + f[2] * a[0],
            f[1] * a[1],
            f[1] * a[2] + f[2] * a[1],
            f[2] * a[2],
            f[3] * a[3],
            f[4] * a[4],
            f[5] * a[5],
        ]
        for n, term in enumerate(terms):
            if not fresh:
                term = acc[1 + n, slot, rows_of(c), :] + term
            if final:
                rows_ref[pl.ds(10 * slot + 1 + n + 8 * c * ROWS, 8, stride=ROWS), :] = scale * term
            else:
                acc[1 + n, slot, rows_of(c), :] = term
        if final:
            term = scale * acc[0, slot, rows_of(c), :]
            rows_ref[pl.ds(10 * slot + 8 * c * ROWS, 8, stride=ROWS), :] = term

    def over(begins, counts, one):
        (a, b), (n, m) = begins, counts
        if n + m:

            def turn(x, carry):
                one(jnp.where(x < n, a + x, b - n + x) if n and m else (a if n else b) + x)
                return carry

            lax.fori_loop(0, n + m, turn, 0)

    def velocity_own(begins, counts, fresh=False, final=False):
        over(begins, counts, lambda x: velocity_plane(DEPTH + x, (0, 1, 2), x, fresh, final))

    def stress_own(step, begins, counts, fresh=False, final=False):
        def one(x):
            for c in range(chunks):
                stress_chunk(DEPTH + x, c, step, x, fresh, final)

        over(begins, counts, one)

    def velocity_rims(step):
        n = DEPTH - 1 - step
        velocity_plane(step, (0,))
        over((step + 1, DEPTH + OWN), (n, n), lambda i: velocity_plane(i, (0, 1, 2)))
        velocity_plane(LENGTH - 1 - step, (1, 2))

    def stress_rims(step):
        n = DEPTH - 1 - step

        def one(i):
            above = i >= DEPTH + OWN
            distance = jnp.where(above, i - DEPTH - OWN, DEPTH - 1 - i)
            for c in range(chunks):
                stress_chunk(i, c, step, rim=(jnp.where(above, 1, 0), RIM_BASE[step] + distance))

        over((step + 1, DEPTH + OWN), (n, n), one)

    if part == "early":
        data_copy = pltpu.make_async_copy(data_in, data, sems.at[HALO_COPIES])

        def start(below, above):
            for copy in halo_copies(state, lines, below, above, sems):
                copy.start()

        by_parity(lambda: start(chip_in, cross_in), lambda: start(cross_in, chip_in))
        data_copy.start()
        draw_image(encoding, cells, image)
        velocity_own((1, 0), (OWN - 2, 0), True)
        for copy in halo_copies(state, lines, cross_in, chip_in, sems):
            copy.wait()
        data_copy.wait()
        whole_lane = lax.broadcasted_iota(jnp.int32, (y_rows, z_rows), 1)
        for side in range(2):
            for n in range(len(RIM_SLOTS)):
                line = lines[side]
                line = pltpu.roll(line, z_rows - RECEIVER_CELLS * n, 1) if n else line
                rim_data[side, n] = jnp.where(whole_lane < RECEIVER_CELLS, line, 0.0)
        velocity_own((0, OWN - 1), (1, 1), True)
        stress_own(0, (1, 0), (OWN - 2, 0), True)
        velocity_own((2, 0), (OWN - 4, 0))
        stress_own(1, (3, 0), (OWN - 6, 0))
        return
    drain_rims(mats, cross_in, chip_in)
    velocity_rims(0)
    stress_rims(0)
    stress_own(0, (0, OWN - 1), (1, 1), True)
    velocity_rims(1)
    velocity_own((0, OWN - 2), (2, 2))
    stress_rims(1)
    stress_own(1, (0, OWN - 3), (3, 3))
    velocity_rims(2)
    velocity_own((0, 0), (OWN, 0))
    stress_rims(2)
    stress_own(2, (0, 0), (OWN, 0))
    velocity_rims(3)
    velocity_own((0, 0), (OWN, 0), False, True)
    copies = []

    def send(source, target):
        copies.append(pltpu.make_async_copy(source, target, sems.at[len(copies)]))
        copies[-1].start()

    for side, out in enumerate((forward, adjoint)):
        send(final_state.at[pl.ds(9 * side, SXX)], out.at[pl.ds(0, SXX)])
    for n in range(2):
        stress_own(3, (n * OWN // 2, 0), (OWN // 2, 0), False, True)
        half = pl.ds(n * ROWS // 2, ROWS // 2)
        send(rows_ref.reshape(y_rows, ROWS, z_rows).at[:, half], packed.at[:, half])
        layers = pl.ds(n * OWN // 2, OWN // 2)
        for side, out in enumerate((forward, adjoint)):
            send(final_state.at[pl.ds(9 * side + SXX, 6), layers], out.at[pl.ds(SXX, 6), layers])
    for copy in copies:
        copy.wait()


def sum_kernel(tiles, out, rows_ref, total, sems):
    parts = tiles.shape[0] // 8
    copies = [
        pltpu.make_async_copy(tiles.at[pl.ds(8 * n, 8)], rows_ref.at[pl.ds(8 * n, 8)], sems.at[n])
        for n in range(parts)
    ]
    for copy in copies:
        copy.start()
    for n in range(parts):
        copies[n].wait()
        for g in range(ROWS // 8):
            rows = pl.ds(8 * g, 8)
            values = [rows_ref[8 * n + j, rows, :] for j in range(8)]
            while len(values) > 1:
                values = [a + b for a, b in zip(values[::2], values[1::2])]
            total[rows, :] = values[0] if n == 0 else total[rows, :] + values[0]
    for m in range(10):
        out[pl.ds(OWN * m, OWN), :] = total[pl.ds(m, OWN, stride=10), :]


def in_vmem(x):
    return pltpu.with_memory_space_constraint(x, VMEM)


def in_hbm(x):
    return pltpu.with_memory_space_constraint(x, pltpu.HBM)


WHOLE = pl.BlockSpec(memory_space=VMEM)
SCALARS = pl.BlockSpec(memory_space=pltpu.SMEM)
ANYWHERE = pl.BlockSpec(memory_space=pl.ANY)
IN_HBM = pl.BlockSpec(memory_space=pltpu.HBM)


def estimate(flops, moved):
    return pl.CostEstimate(flops=flops, bytes_accessed=moved, transcendentals=0)


def run_phase(part, scalars, state, middle, far):
    y_rows, z_rows = state.shape[2:]
    count = len(scalars)
    outs = [VMEM(state.shape, jnp.float32), VMEM((10, OWN, y_rows, z_rows), jnp.float32)]
    aliases = {count: 0}
    if part == "early":
        outs += [
            VMEM((LENGTH, y_rows, z_rows), jnp.float32),
            VMEM((2, len(RIM_SLOTS), y_rows, z_rows), jnp.float32),
            VMEM((STEPS, OWN, y_rows, z_rows), jnp.float32),
        ]
        out_specs = [WHOLE] * len(outs)
        scratch = [VMEM((2, y_rows, z_rows), jnp.float32), pltpu.SemaphoreType.DMA((HALO_COPIES + 1,))]
    else:
        outs += [
            VMEM((10, LENGTH, y_rows, z_rows), jnp.float32),
            pltpu.HBM((state.shape[0] // 2, OWN, y_rows, z_rows), jnp.float32),
            pltpu.HBM((state.shape[0] // 2, OWN, y_rows, z_rows), jnp.float32),
            pltpu.HBM((y_rows, ROWS, z_rows), jnp.float32),
        ]
        aliases.update({count + 1: 1, count + 2: 2})
        scratch = [
            VMEM((y_rows * ROWS, z_rows), jnp.float32),
            VMEM((state.shape[0], OWN, y_rows, z_rows), jnp.float32),
            pltpu.SemaphoreType.DMA((8,)),
        ]
        out_specs = [WHOLE] * 3 + [IN_HBM] * 3
    cells = 12 * y_rows * z_rows
    return pl.pallas_call(
        functools.partial(phase_kernel, part, y_rows, z_rows),
        out_shape=tuple(outs),
        in_specs=[SCALARS] * count + [WHOLE] * (1 + len(middle)) + [ANYWHERE] * len(far),
        out_specs=tuple(out_specs),
        scratch_shapes=scratch,
        input_output_aliases=aliases,
        cost_estimate=estimate(160 * cells, 100 * cells),
        compiler_params=pltpu.CompilerParams(vmem_limit_bytes=6 << 20),
        name="steps_" + part,
    )(*scalars, in_vmem(state), *[in_vmem(x) for x in middle], *far)


def swap_across(value):
    peers = lax.axis_size("slab")
    return lax.ppermute(value, "slab", [p for i in range(1, peers - 1, 2) for p in ((i, i + 1), (i + 1, i))])


def swap_on_chip(value):
    peers = lax.axis_size("slab")
    return lax.ppermute(value, "slab", [p for i in range(0, peers, 2) for p in ((i, i + 1), (i + 1, i))])


def body(
    forward_state,
    adjoint_state,
    materials,
    wavelet,
    encoding,
    source_cells,
    receiver_depth,
    receiver_data,
):
    _, comps, own, y_rows, z_rows = forward_state.shape
    shots = lax.axis_size("shot")
    small = pltpu.CompilerParams(vmem_limit_bytes=2 << 20)

    copies = pl.pallas_call(
        spread_kernel,
        out_shape=pltpu.HBM((shots, ROWS, z_rows), jnp.float32),
        in_specs=[IN_HBM],
        out_specs=IN_HBM,
        scratch_shapes=[
            VMEM((ROWS, z_rows), jnp.float32),
            pltpu.SemaphoreType.DMA,
            pltpu.SemaphoreType.DMA((shots,)),
        ],
        cost_estimate=estimate(1000, 4 * shots * ROWS * z_rows),
        compiler_params=small,
        name="spread",
    )(in_hbm(materials.reshape(ROWS, z_rows)))
    gathered = lax.all_to_all(copies, "shot", split_axis=0, concat_axis=0, tiled=True)

    z_at = lax.broadcasted_iota(jnp.int32, (own, y_rows, z_rows), 2)
    probe = z_at == receiver_depth[:, :, None]
    data = jnp.where(probe[None], receiver_data[0][:, :, :, None], 0.0)

    payload = pltpu.HBM((PAYLOAD, y_rows, z_rows), jnp.float32)
    moved = 8 * comps * own * y_rows * z_rows
    fields = [in_hbm(forward_state[0]), in_hbm(adjoint_state[0])]
    cross, chip = pl.pallas_call(
        stage_kernel,
        out_shape=(payload, payload),
        in_specs=[IN_HBM, IN_HBM, WHOLE],
        out_specs=(IN_HBM, IN_HBM),
        scratch_shapes=[
            VMEM((2 * comps, own, y_rows, z_rows), jnp.float32),
            VMEM((2, y_rows, z_rows), jnp.float32),
            pltpu.SemaphoreType.DMA((4 * comps + 2,)),
        ],
        cost_estimate=estimate(1000, moved),
        compiler_params=pltpu.CompilerParams(vmem_limit_bytes=4 << 20),
        name="stage",
    )(*fields, in_vmem(data))
    cross, chip = swap_across(cross), swap_on_chip(chip)

    chunks = y_rows // 8
    rim = VMEM((RIM_PLANES, y_rows, z_rows), jnp.float32)
    mats, far, near, state = pl.pallas_call(
        turn_kernel,
        out_shape=(
            VMEM((10, LENGTH, y_rows, z_rows), jnp.float32),
            rim,
            rim,
            VMEM((2 * comps, LENGTH, y_rows, z_rows), jnp.float32),
        ),
        in_specs=[ANYWHERE, IN_HBM, IN_HBM],
        out_specs=(WHOLE,) * 4,
        scratch_shapes=[
            VMEM((chunks, 8 * ROWS, z_rows), jnp.float32),
            pltpu.SemaphoreType.DMA((chunks + 2 * comps,)),
        ],
        cost_estimate=estimate(1000, 8 * shots * ROWS * z_rows),
        compiler_params=pltpu.CompilerParams(vmem_limit_bytes=4 << 20),
        name="turn",
    )(gathered.reshape(chunks, 8 * ROWS, z_rows), *fields)
    far, near = swap_across(far), swap_on_chip(near)
    scalars = (wavelet, encoding, source_cells)
    state, acc, image, rim_data, data = run_phase("early", scalars, state, [mats], [cross, chip, data])
    middle = [acc, mats, far, near, image, rim_data, data]
    _, _, _, forward_out, adjoint_out, packed = run_phase("rest", (wavelet,), state, middle, [])

    tiles = lax.all_to_all(packed, "shot", 0, 0, tiled=True)
    gradient = pl.pallas_call(
        sum_kernel,
        out_shape=jax.ShapeDtypeStruct((ROWS, z_rows), jnp.float32),
        in_specs=[ANYWHERE],
        out_specs=WHOLE,
        scratch_shapes=[
            VMEM((shots, ROWS, z_rows), jnp.float32),
            VMEM((ROWS, z_rows), jnp.float32),
            pltpu.SemaphoreType.DMA((shots // 8,)),
        ],
        cost_estimate=estimate(shots * ROWS * z_rows, 4 * shots * ROWS * z_rows),
        compiler_params=pltpu.CompilerParams(vmem_limit_bytes=4 << 20),
        name="sum",
    )(tiles)
    gradient = gradient.reshape(10, own, 1, z_rows)
    return forward_out[None], adjoint_out[None], gradient


def solution(mesh):
    state_spec = P("shot", None, "slab", None, None)
    return jax.shard_map(
        body,
        mesh=mesh,
        in_specs=(
            state_spec,
            state_spec,
            P(None, "slab", "shot", None),
            P(),
            P("shot", None),
            P("shot", None),
            P("slab", None),
            P("shot", None, "slab", None),
        ),
        out_specs=(state_spec, state_spec, P(None, "slab", "shot", None)),
        check_vma=False,
    )
```
